32 devices in a mesh: gx: 8 (over z, y), gy: 4 (over x, core).
Axes of the slice: x: 2, y: 2, z: 4, core: 2. Of those that a mesh axis runs over, the one named last changes fastest.
Arguments:
- ensemble_state: float32 [64, 64, 4096], P(None, 'gx', 'gy'), may hold values from -32 to 32, as said below
- courant_rows: float32 [64, 4096], P('gx', 'gy'), may hold values from -0.4 to 0.4
- courant_cols: float32 [64, 4096], P('gx', 'gy'), may hold values from -0.4 to 0.4
- diffusivity: float32 [64, 4096], P('gx', 'gy'), may hold values from 0.02 to 0.05
- owner_tile: int32 [2], replicated, may hold values from 0 to 31
- target_row: int32 [2, 64], replicated, may hold values from 0 to 7
- target_col: int32 [2, 64], replicated, may hold values from 0 to 1023
- serial_order: int32 [2, 64], replicated, may hold values from 0 to 63, each once within a row
- taper_radius: int32 [2, 64], replicated, may hold values from 64 to 128
- observed: float32 [2, 64], replicated, may hold values from -6 to 6
- error_variance: float32 [2, 64], replicated, may hold values from 0.2 to 2
Outputs:
- analysis: float32 [64, 64, 4096], P(None, 'gx', 'gy')
The draws below stay inside these ranges and needn't reach their ends.
Inputs may be any that keep to these rules, and one draw needn't show every extreme that they name: `ensemble_state`: the prior ensemble's spread differs from cell to cell.
All inputs are finite; a program needn't handle non-finite values.
Results may differ from the reference program's by a relative error of at most 0.0001.
Values sent between devices are 32-bit elements; how exact they have to be, the bound alone decides.
A program may use at most 128 MiB of HBM per device.

```python
import math
import jax
import jax.numpy as jnp
from jax import lax

MEMBERS = 64
TILE_ROWS = 8
TILE_COLS = 1024
BATCHES = 2
BATCH_OBS = 64
TILES_Y = 4
TILES = 32
GRID_ROWS = 64
GRID_COLS = 4096


def draw_ensemble_state(key, part):
    subkeys = jax.random.split(key, 4)
    base_field = jnp.clip(jax.random.normal(subkeys[0], (1, GRID_ROWS, GRID_COLS), jnp.float32), -3.0, 3.0)
    spread_log = jax.random.uniform(subkeys[1], (1, GRID_ROWS, GRID_COLS), jnp.float32, math.log(0.3), math.log(3.0))
    member_scale = jax.random.uniform(subkeys[2], (MEMBERS, 1, 1), jnp.float32, 0.6, 1.6)
    noise_draw = jnp.clip(jax.random.normal(subkeys[3], (MEMBERS, GRID_ROWS, GRID_COLS), jnp.float32), -4.0, 4.0)
    return base_field + jnp.exp(spread_log) * member_scale * noise_draw


def place_ends(entries, stream_key, least, high):
    index_at = [jax.random.randint(jax.random.fold_in(stream_key, axis), (), 0, length) for axis, length in enumerate(entries.shape)]
    main_axis = entries.shape.index(max(entries.shape))
    beside = index_at[:main_axis] + [(index_at[main_axis] + 1) % entries.shape[main_axis]] + index_at[main_axis + 1:]
    return entries.at[tuple(index_at)].set(least).at[tuple(beside)].set(high)


def steps_of(own_key, dims, pieces, least, high):
    level, own = 1.0, jax.random.fold_in(own_key, 6)
    for axis_at, shards_of in pieces:
        steps = jnp.exp(jax.random.uniform(jax.random.fold_in(own, axis_at), (shards_of,), jnp.float32, least / len(pieces), high / len(pieces)))
        level = level * jnp.repeat(steps, dims[axis_at] // shards_of).reshape([-1 if axis == axis_at else 1 for axis in range(len(dims))])
    return level


def scatter_about(own_key, dims, scale, limit, dtype=jnp.bfloat16):
    values = jax.random.normal(own_key, dims, jnp.float32) * scale
    return jnp.minimum(jnp.maximum(values, -limit), limit).astype(dtype)


def setup_inputs(seed: int = 0) -> dict:
    streams_of = jax.random.split(jax.random.key(seed), 12)
    return {
        "ensemble_state": draw_ensemble_state(jax.random.fold_in(streams_of[11], 71), 0),
        "courant_rows": jnp.clip(jax.random.uniform(streams_of[1], (GRID_ROWS, GRID_COLS), jnp.float32, -0.4, 0.4) * steps_of(streams_of[1], (GRID_ROWS, GRID_COLS), ((0, 8), (1, 4)), -0.4, 0.0), -0.4, 0.4),
        "courant_cols": jnp.clip(jax.random.uniform(streams_of[2], (GRID_ROWS, GRID_COLS), jnp.float32, -0.4, 0.4) * steps_of(streams_of[2], (GRID_ROWS, GRID_COLS), ((0, 8), (1, 4)), -0.4, 0.0), -0.4, 0.4),
        "diffusivity": jnp.clip(jnp.exp(math.log(0.05) - 0.91629077 * jax.random.uniform(streams_of[3], (GRID_ROWS, GRID_COLS), jnp.float32) ** steps_of(streams_of[3], (GRID_ROWS, GRID_COLS), ((0, 8), (1, 4)), -0.2, 0.2)), 0.02, 0.05),
        "owner_tile": jax.random.randint(streams_of[4], (BATCHES,), 0, TILES).astype(jnp.int32),
        "target_row": place_ends(jax.random.randint(streams_of[5], (BATCHES, BATCH_OBS), 0, TILE_ROWS), jax.random.fold_in(streams_of[5], 1), 0, TILE_ROWS - 1).astype(jnp.int32),
        "target_col": place_ends(jax.random.randint(streams_of[6], (BATCHES, BATCH_OBS), 0, TILE_COLS), jax.random.fold_in(streams_of[6], 1), 0, TILE_COLS - 1).astype(jnp.int32),
        "serial_order": jax.vmap(lambda own: jax.random.permutation(own, BATCH_OBS))(jax.random.split(streams_of[7], BATCHES)).reshape((BATCHES, BATCH_OBS)).astype(jnp.int32),
        "taper_radius": place_ends(jax.random.randint(streams_of[8], (BATCHES, BATCH_OBS), GRID_ROWS, 2 * GRID_ROWS + 1), jax.random.fold_in(streams_of[8], 1), GRID_ROWS, 2 * GRID_ROWS).astype(jnp.int32),
        "observed": scatter_about(streams_of[9], (BATCHES, BATCH_OBS), 1.5, 6.0, jnp.float32),
        "error_variance": jnp.clip(jnp.exp(jax.random.uniform(streams_of[10], (BATCHES, BATCH_OBS), jnp.float32, math.log(0.2), math.log(2.0))), 0.2, 2.0),
    }


def advance(extended, courant_rows, courant_cols, diffusivity):
    center = extended[:, 1:-1, 1:-1]
    upper_cells = extended[:, :-2, 1:-1]
    lower_cells = extended[:, 2:, 1:-1]
    left_cells = extended[:, 1:-1, :-2]
    right_cells = extended[:, 1:-1, 2:]
    flow_rows = jnp.maximum(courant_rows, 0.0) * (center - upper_cells) + jnp.minimum(courant_rows, 0.0) * (lower_cells - center)
    flow_cols = jnp.maximum(courant_cols, 0.0) * (center - left_cells) + jnp.minimum(courant_cols, 0.0) * (right_cells - center)
    spread = diffusivity * (upper_cells + lower_cells + left_cells + right_cells - 4.0 * center)
    return center - flow_rows - flow_cols + spread

def taper_weight(row_gap, col_gap, radius):
    scaled = (row_gap * row_gap + col_gap * col_gap) / (radius * radius)
    return jnp.square(jnp.maximum(1.0 - scaled, 0.0))

def increments(column, observed_value, error_value):
    members = column.shape[0]
    average = jnp.mean(column)
    anomaly = column - average
    variance = jnp.sum(anomaly * anomaly) / (members - 1) + 1e-05
    combined = variance + error_value
    posterior = (error_value * average + variance * observed_value) / combined
    increment = posterior + jnp.sqrt(error_value / combined) * anomaly - column
    return (anomaly, increment, variance)

def reference(ensemble_state, courant_rows, courant_cols, diffusivity, owner_tile, target_row, target_col, serial_order, taper_radius, observed, error_variance):
    analysis = ensemble_state
    for substep in range(2):
        extended = jnp.pad(analysis, ((0, 0), (1, 1), (1, 1)))
        analysis = advance(extended, courant_rows, courant_cols, diffusivity)
    members = analysis.shape[0]
    window_width = TILE_COLS + 4 * GRID_ROWS
    for batch_index in range(BATCHES):
        owner = owner_tile[batch_index]
        obs_rows = owner // TILES_Y * TILE_ROWS + target_row[batch_index]
        obs_cols = owner % TILES_Y * TILE_COLS + target_col[batch_index]
        first_col = jnp.clip(owner % TILES_Y * TILE_COLS - 2 * GRID_ROWS, 0, GRID_COLS - window_width).astype(jnp.int32)
        corner = (jnp.int32(0), jnp.int32(0), first_col)
        window = lax.dynamic_slice(analysis, corner, (members, GRID_ROWS, window_width))
        priors = analysis[:, obs_rows, obs_cols]
        grid_rows = jnp.arange(GRID_ROWS).astype(jnp.float32)[:, None]
        grid_cols = (first_col + jnp.arange(window_width)).astype(jnp.float32)[None, :]
        rows_float = obs_rows.astype(jnp.float32)
        cols_float = obs_cols.astype(jnp.float32)

        def assimilate(carry, number):
            window, priors = carry
            which = serial_order[batch_index, number]
            anomaly, increment, variance = increments(priors[:, which], observed[batch_index, which], error_variance[batch_index, which])
            radius = taper_radius[batch_index, which].astype(jnp.float32)
            here_row = rows_float[which]
            here_col = cols_float[which]
            point_weight = taper_weight(rows_float - here_row, cols_float - here_col, radius)
            centred = priors - lax.optimization_barrier(jnp.mean(priors, axis=0))
            covariance = lax.optimization_barrier(jnp.sum(centred * anomaly[:, None], axis=0)) / (members - 1)
            priors = priors + increment[:, None] * (point_weight * covariance / variance)[None, :]
            window_centred = window - lax.optimization_barrier(jnp.mean(window, axis=0))
            cell_cov = lax.optimization_barrier(jnp.sum(window_centred * anomaly[:, None, None], axis=0)) / (members - 1)
            cell_weight = taper_weight(grid_rows - here_row, grid_cols - here_col, radius)
            window = window + increment[:, None, None] * (cell_weight * cell_cov / variance)[None]
            return ((window, priors), None)
        (window, priors), unused = lax.scan(assimilate, (window, priors), jnp.arange(BATCH_OBS))
        analysis = lax.dynamic_update_slice(analysis, window, corner)
    return analysis
```

```python
import functools
import jax
import jax.numpy as jnp
from jax import lax
from jax.experimental import pallas as pl
from jax.experimental.pallas import tpu as pltpu
from jax.sharding import PartitionSpec as P

MESH = pl.DeviceIdType.MESH
VLIMIT = 48 * 1024 * 1024
F32 = jnp.float32
BF16 = jnp.bfloat16
CHUNK = 512


def advect_kernel(nx, ny, state_in, cr_ref, cc_ref, k_ref, out, state, once, coef, row_send, row_recv, col_recv,
                  row_ss, row_rs, col_ss, col_rs):
    members = state_in.shape[0] // 8
    cols = state_in.shape[1]
    blocks = cols // 128
    gx = lax.axis_index("gx")
    gy = lax.axis_index("gy")
    has = (gx > 0, gx < nx - 1, gy > 0, gy < ny - 1)
    peer = (
        (jnp.maximum(gx - 1, 0), gy),
        (jnp.minimum(gx + 1, nx - 1), gy),
        (gx, jnp.maximum(gy - 1, 0)),
        (gx, jnp.minimum(gy + 1, ny - 1)),
    )
    barrier = pltpu.get_barrier_semaphore()
    for d in range(4):
        @pl.when(has[d])
        def _(d=d):
            pl.semaphore_signal(barrier, inc=1, device_id=peer[d], device_id_type=MESH)

    def row_copy(phase, d):
        return pltpu.make_async_remote_copy(
            row_send.at[phase, d], row_recv.at[phase, 1 - d],
            row_ss.at[phase, d], row_rs.at[phase, 1 - d],
            device_id=peer[d], device_id_type=MESH)

    def col_copy(phase, d, source):
        block = 0 if d == 0 else blocks - 1
        return pltpu.make_async_remote_copy(
            source.at[block], col_recv.at[phase, 1 - d],
            col_ss.at[phase, d], col_rs.at[phase, 1 - d],
            device_id=peer[2 + d], device_id_type=MESH)

    def pack(phase, source):
        for j in range(blocks):
            lanes = slice(j * 128, (j + 1) * 128)
            row_send[phase, 0, :, lanes] = source[j, pl.ds(0, members, stride=8), :]
            row_send[phase, 1, :, lanes] = source[j, pl.ds(7, members, stride=8), :]

    for j in range(blocks):
        state[j] = state_in[:, j * 128:(j + 1) * 128]
    pack(0, state)
    pl.semaphore_wait(barrier, sum(h.astype(jnp.int32) for h in has))

    def send(phase, source):
        for d in range(2):
            @pl.when(has[d])
            def _(d=d):
                row_copy(phase, d).start()
        for d in range(2):
            @pl.when(has[2 + d])
            def _(d=d):
                col_copy(phase, d, source).start()

    send(0, state)
    for d in range(2):
        @pl.when(jnp.logical_not(has[d]))
        def _(d=d):
            for phase in range(2):
                row_recv[phase, d] = jnp.zeros((members, cols), F32)

        @pl.when(jnp.logical_not(has[2 + d]))
        def _(d=d):
            for phase in range(2):
                col_recv[phase, d] = jnp.zeros((members * 8, 128), F32)
    cr, cc, kk = cr_ref[...], cc_ref[...], k_ref[...]
    pr, mr = jnp.maximum(cr, 0.0), jnp.minimum(cr, 0.0)
    pc, mc = jnp.maximum(cc, 0.0), jnp.minimum(cc, 0.0)
    coef[0] = 1.0 - pr + mr - pc + mc - 4.0 * kk
    coef[1] = pr + kk
    coef[2] = kk - mr
    coef[3] = pc + kk
    coef[4] = kk - mc

    def receive(phase, source):
        for d in range(2):
            @pl.when(has[d])
            def _(d=d):
                row_copy(phase, 1 - d).wait_recv()
        for d in range(2):
            @pl.when(has[2 + d])
            def _(d=d):
                col_copy(phase, 1 - d, source).wait_recv()

    def substep(phase, source, target):
        top = lax.broadcasted_iota(jnp.int32, (8, cols), 0) == 0
        bottom = lax.broadcasted_iota(jnp.int32, (8, cols), 0) == 7

        def member(e, carry):
            rows = pl.ds(pl.multiple_of(e * 8, 8), 8)
            center = jnp.concatenate([source[j, rows, :] for j in range(blocks)], axis=1)
            left = pltpu.roll(jnp.concatenate([col_recv[phase, 0, rows, :], center], axis=1), 1, 1)[:, 128:]
            right = pltpu.roll(
                jnp.concatenate([center, col_recv[phase, 1, rows, :]], axis=1), cols + 127, 1)[:, :cols]
            up = jnp.where(top, row_recv[phase, 0, pl.ds(e, 1), :], pltpu.roll(center, 1, 0))
            down = jnp.where(bottom, row_recv[phase, 1, pl.ds(e, 1), :], pltpu.roll(center, 7, 0))
            new = (coef[0] * center + coef[1] * up + coef[2] * down
                   + coef[3] * left + coef[4] * right)
            for j in range(blocks):
                target[j, rows, :] = new[:, j * 128:(j + 1) * 128]
            return carry

        lax.fori_loop(0, members, member, 0)

    receive(0, state)
    substep(0, state, once)
    pack(1, once)
    send(1, once)
    receive(1, once)
    substep(1, once, out)
    for phase, source in ((0, state), (1, once)):
        for d in range(2):
            @pl.when(has[d])
            def _(d=d, phase=phase):
                row_copy(phase, d).wait_send()

            @pl.when(has[2 + d])
            def _(d=d, phase=phase, source=source):
                col_copy(phase, d, source).wait_send()


def advect(nx, ny, state, cr, cc, kk):
    size, cols = state.shape
    members = size // 8
    vmem = pl.BlockSpec(memory_space=pltpu.VMEM)
    return pl.pallas_call(
        functools.partial(advect_kernel, nx, ny),
        out_shape=jax.ShapeDtypeStruct((cols // 128, size, 128), F32),
        in_specs=[vmem] * 4,
        out_specs=vmem,
        scratch_shapes=[
            pltpu.VMEM((cols // 128, size, 128), F32),
            pltpu.VMEM((cols // 128, size, 128), F32),
            pltpu.VMEM((5, 8, cols), F32),
            pltpu.VMEM((2, 2, members, cols), F32),
            pltpu.VMEM((2, 2, members, cols), F32),
            pltpu.VMEM((2, 2, size, 128), F32),
            pltpu.SemaphoreType.DMA((2, 2)),
            pltpu.SemaphoreType.DMA((2, 2)),
            pltpu.SemaphoreType.DMA((2, 2)),
            pltpu.SemaphoreType.DMA((2, 2)),
        ],
        compiler_params=pltpu.CompilerParams(
            collective_id=0, has_side_effects=True, vmem_limit_bytes=VLIMIT),
        name="advect",
    )(state, cr, cc, kk)


def gather_kernel(ny, owner, trow, tcol, order, radius, obs, err, adv, priors_out, params_out):
    members = adv.shape[1] // 8
    tile_cols = adv.shape[0] * 128
    count = trow.shape[1]
    me = lax.axis_index("gx") * ny + lax.axis_index("gy")
    lane = lax.broadcasted_iota(jnp.int32, (1, 128), 1)
    lanes = lax.broadcasted_iota(jnp.int32, (members, 128), 1)
    sub = lax.broadcasted_iota(jnp.int32, (8, 128), 0)
    lane8 = lax.broadcasted_iota(jnp.int32, (8, 128), 1)
    unroll = 16
    acc = jnp.zeros((members, 128), F32)
    par = jnp.zeros((8, 128), F32)
    for b in range(2):
        own = owner[b]
        mine = own == me

        def body(blk, carry, b=b, own=own, mine=mine):
            acc, par = carry
            for i in range(unroll):
                t = blk * unroll + i
                k = order[b, t]
                r = trow[b, k]
                c = tcol[b, k]
                block = lax.div(c, jnp.int32(128))
                inner = c - block * 128
                at = b * count + t
                x = adv[block, pl.ds(r, members, stride=8), :]
                x = pltpu.roll(x, lax.rem(at - inner + 128, jnp.int32(128)), 1)
                acc = jnp.where(lanes == jnp.where(mine, at, -1), x, acc)
                grow = (lax.div(own, jnp.int32(ny)) * 8 + r).astype(F32)
                gcol = (lax.rem(own, jnp.int32(ny)) * tile_cols + c).astype(F32)
                rad = radius[b, k].astype(F32)
                new = jnp.where(
                    sub == 0, grow,
                    jnp.where(sub == 1, gcol, jnp.where(sub == 2, rad, jnp.where(sub == 3, obs[b, k], err[b, k]))))
                par = jnp.where(lane8 == at, new, par)
            return acc, par

        acc, par = lax.fori_loop(0, count // unroll, body, (acc, par))
    priors_out[...] = acc
    params_out[...] = par


def gather(ny, smalls, adv):
    members = adv.shape[1] // 8
    vmem = pl.BlockSpec(memory_space=pltpu.VMEM)
    smem = pl.BlockSpec(memory_space=pltpu.SMEM)
    return pl.pallas_call(
        functools.partial(gather_kernel, ny),
        out_shape=(jax.ShapeDtypeStruct((members, 128), F32), jax.ShapeDtypeStruct((8, 128), F32)),
        in_specs=[smem] * 7 + [vmem],
        out_specs=(vmem, vmem),
        compiler_params=pltpu.CompilerParams(vmem_limit_bytes=VLIMIT),
        name="gather",
    )(*smalls, adv)


def sum_kernel(nx, ny, x, out, acc, recv, ss, rs):
    gx = lax.axis_index("gx")
    gy = lax.axis_index("gy")
    peers = []
    bit = 1
    while bit < ny:
        peers.append((gx, gy + bit - 2 * bit * ((gy // bit) % 2)))
        bit *= 2
    bit = 1
    while bit < nx:
        peers.append((gx + bit - 2 * bit * ((gx // bit) % 2), gy))
        bit *= 2
    barrier = pltpu.get_barrier_semaphore()
    for p in peers:
        pl.semaphore_signal(barrier, inc=1, device_id=p, device_id_type=MESH)
    pl.semaphore_wait(barrier, len(peers))
    copies = []
    for s, p in enumerate(peers):
        source = x if s == 0 else acc.at[s]
        copy = pltpu.make_async_remote_copy(
            source, recv.at[s], ss.at[s], rs.at[s], device_id=p, device_id_type=MESH)
        copy.start()
        copies.append(copy)
        copy.wait_recv()
        total = source[...] + recv[s]
        if s + 1 < len(peers):
            acc[s + 1] = total
        else:
            out[...] = total
    for copy in copies:
        copy.wait_send()


def all_sum(nx, ny, x):
    stages = (nx.bit_length() - 1) + (ny.bit_length() - 1)
    vmem = pl.BlockSpec(memory_space=pltpu.VMEM)
    return pl.pallas_call(
        functools.partial(sum_kernel, nx, ny),
        out_shape=jax.ShapeDtypeStruct(x.shape, F32),
        in_specs=[vmem],
        out_specs=vmem,
        scratch_shapes=[
            pltpu.VMEM((stages,) + x.shape, F32),
            pltpu.VMEM((stages,) + x.shape, F32),
            pltpu.SemaphoreType.DMA((stages,)),
            pltpu.SemaphoreType.DMA((stages,)),
        ],
        compiler_params=pltpu.CompilerParams(
            collective_id=1, has_side_effects=True, vmem_limit_bytes=VLIMIT),
        name="all_sum",
    )(x)


def split(x):
    hi = x.astype(BF16)
    return hi, (x - hi.astype(F32)).astype(BF16)


def chain_kernel(priors, params, anomalies_out, means_out):
    members, lanes = priors.shape
    lane = lax.broadcasted_iota(jnp.int32, (1, lanes), 1)
    x = priors[...]
    mean = jnp.mean(x, axis=0, keepdims=True)
    a = x - mean
    row, col, rad = params[0:1, :], params[1:2, :], params[2:3, :]
    inv_rad2 = 1.0 / (rad * rad)
    obs, err = params[3:4, :], params[4:5, :]
    for k in range(lanes):
        def pick(v, k=k):
            return jnp.broadcast_to(v[:, k:k + 1], v.shape)
        dr, dc = row - pick(row), col - pick(col)
        taper = jnp.square(jnp.maximum(1.0 - (dr * dr + dc * dc) * pick(inv_rad2), 0.0))
        taper = jnp.where(lane > k, taper, 0.0) * (1.0 / (members - 1))
        r, o = pick(err), pick(obs)
        ak = pick(a)
        mk = pick(mean)
        cov = jnp.sum(a * ak, axis=0, keepdims=True)
        s2 = jnp.sum(ak * ak, axis=0, keepdims=True) * (1.0 / (members - 1)) + 1e-05
        inv = 1.0 / (s2 + r)
        shift = s2 * (o - mk) * inv
        beta = jnp.sqrt(r * inv) - 1.0
        w = taper * cov / s2
        a = a + (w * beta) * ak
        mean = mean + w * shift
    anomalies_out[...] = a
    means_out[...] = jnp.broadcast_to(mean, (8, lanes))


def chain(priors, params):
    vmem = pl.BlockSpec(memory_space=pltpu.VMEM)
    return pl.pallas_call(
        chain_kernel,
        out_shape=(jax.ShapeDtypeStruct(priors.shape, F32), jax.ShapeDtypeStruct((8, 128), F32)),
        in_specs=[vmem] * 2,
        out_specs=(vmem, vmem),
        compiler_params=pltpu.CompilerParams(vmem_limit_bytes=VLIMIT),
        name="chain",
    )(priors, params)


def apply_kernel(adv, anomalies, means, params, final, out, coupling, weights, tapers, lhs1, lhs2):
    members, lanes = anomalies.shape
    blocks = adv.shape[0]
    cols = blocks * 128
    count = lanes // 2
    width = CHUNK // 128
    row_base = lax.axis_index("gx") * 8
    col_base = lax.axis_index("gy") * cols
    a = anomalies[...]
    mean = means[0:1, :]
    col, rad = params[1:2, :], params[2:3, :]
    obs, err = params[3:4, :], params[4:5, :]
    s2 = jnp.sum(a * a, axis=0, keepdims=True) * (1.0 / (members - 1)) + 1e-05
    inv = 1.0 / (s2 + err)
    shift = s2 * (obs - mean) * inv
    beta = jnp.sqrt(err * inv) - 1.0
    delta = beta * a
    pad = jnp.zeros((lanes - members, lanes), F32)
    at = jnp.concatenate([a, pad], axis=0).T
    g = jnp.dot(at, jnp.concatenate([delta, pad], axis=0), precision=lax.Precision.HIGHEST,
                preferred_element_type=F32)
    for s in range(lanes):
        b = s // count
        coupling[s] = jnp.broadcast_to(g[b * count:(b + 1) * count, s:s + 1], (count, lanes))
    ahi, alo = split(a)
    ahi, alo = ahi.astype(F32), alo.astype(F32)
    stacked = jnp.concatenate([ahi, ahi, alo, jnp.zeros_like(alo)], axis=0)
    lhs1[...] = stacked.T.astype(BF16)
    dd = delta + shift
    dhi, dlo = split(dd)
    dhi, dlo = dhi.astype(F32), dlo.astype(F32)
    for b in range(2):
        part = slice(b * count, (b + 1) * count)
        lhs2[b] = jnp.concatenate(
            [dhi[:, part], dhi[:, part], dlo[:, part], jnp.zeros((members, count), F32)], axis=1).astype(BF16)
    pt = jnp.concatenate(
        [params[0:3, :], 1.0 / (s2 * (members - 1)), jnp.zeros((lanes - 4, lanes), F32)], axis=0).T
    lane = lax.broadcasted_iota(jnp.int32, (1, lanes), 1)
    big = 1e9
    low, high = [], []
    for b in range(2):
        inside = (lane >= b * count) & (lane < (b + 1) * count)
        low.append(jnp.min(jnp.where(inside, col - rad, big)))
        high.append(jnp.max(jnp.where(inside, col + rad, -big)))
    cells = lax.broadcasted_iota(jnp.int32, (count, CHUNK), 1)
    chunks = cols // CHUNK

    def step(number, carry):
        r = number // chunks
        chunk = number % chunks
        start = pl.multiple_of(chunk * CHUNK, CHUNK)
        places = [(chunk * width + j, pl.ds(r, members, stride=8)) for j in range(width)]
        for place in places:
            out[place] = adv[place]
        first = (col_base + start).astype(F32)
        grow = (row_base + r).astype(F32)
        for b in range(2):
            part = slice(b * count, (b + 1) * count)

            @pl.when((first + (CHUNK - 1.0) > low[b]) & (first < high[b]))
            def _(b=b, part=part):
                x = jnp.concatenate([out[place] for place in places], axis=1)
                dr = pt[part, 0:1] - grow
                dc = (cells + (col_base + start)).astype(F32) - pt[part, 1:2]
                inv2 = 1.0 / (pt[part, 2:3] * pt[part, 2:3])
                t = jnp.maximum(1.0 - (dr * dr + dc * dc) * inv2, 0.0)
                tapers[...] = t * t * pt[part, 3:4]
                xhi, xlo = split(x)
                carried = jnp.dot(
                    lhs1[part, :], jnp.concatenate([xhi, xlo, xhi, jnp.zeros_like(xhi)], axis=0),
                    preferred_element_type=F32)
                groups = [carried[i * 8:(i + 1) * 8, :] for i in range(count // 8)]
                for k in range(count):
                    gi, si = k // 8, k % 8
                    w = groups[gi][si:si + 1, :] * tapers[k:k + 1, :]
                    weights[k:k + 1, :] = w
                    first_group = gi if si < 7 else gi + 1
                    for gj in range(first_group, count // 8):
                        c = coupling[b * count + k, gj * 8:(gj + 1) * 8, :]
                        c = jnp.concatenate([c] * (CHUNK // 128), axis=1)
                        groups[gj] = groups[gj] + c * w
                whi, wlo = split(weights[...])
                x = x + jnp.dot(
                    lhs2[b], jnp.concatenate([whi, wlo, whi, jnp.zeros_like(whi)], axis=0),
                    preferred_element_type=F32)
                for j, place in enumerate(places):
                    out[place] = x[:, j * 128:(j + 1) * 128]
        return carry

    lax.fori_loop(0, 8 * chunks, step, 0)
    for j in range(blocks):
        final[:, j * 128:(j + 1) * 128] = out[j]


def apply(adv, anomalies, means, params):
    members, lanes = anomalies.shape
    count = lanes // 2
    vmem = pl.BlockSpec(memory_space=pltpu.VMEM)
    return pl.pallas_call(
        apply_kernel,
        out_shape=jax.ShapeDtypeStruct((adv.shape[1], adv.shape[0] * 128), F32),
        in_specs=[vmem] * 4,
        out_specs=vmem,
        scratch_shapes=[
            pltpu.VMEM(adv.shape, F32),
            pltpu.VMEM((lanes, count, lanes), F32),
            pltpu.VMEM((count, CHUNK), F32),
            pltpu.VMEM((count, CHUNK), F32),
            pltpu.VMEM((lanes, 256), BF16),
            pltpu.VMEM((2, members, 256), BF16),
        ],
        compiler_params=pltpu.CompilerParams(vmem_limit_bytes=VLIMIT),
        name="apply",
    )(adv, anomalies, means, params)


def solution(mesh):
    nx, ny = mesh.shape["gx"], mesh.shape["gy"]

    def local(state, cr, cc, kk, owner, trow, tcol, order, radius, obs, err):
        members, rows, cols = state.shape
        adv = advect(nx, ny, state.reshape(members * rows, cols), cr, cc, kk)
        priors, params = gather(ny, (owner, trow, tcol, order, radius, obs, err), adv)
        priors = all_sum(nx, ny, priors)
        anomalies, means = chain(priors, params)
        out = apply(adv, anomalies, means, params)
        return out.reshape(members, rows, cols)

    split_spec = P(None, "gx", "gy")
    cell = P("gx", "gy")
    return jax.shard_map(
        local, mesh=mesh, in_specs=(split_spec,) + (cell,) * 3 + (P(),) * 7, out_specs=split_spec, check_vma=False)
```

```python
import functools
import jax
import jax.numpy as jnp
from jax import lax
from jax.experimental import pallas as pl
from jax.experimental.pallas import tpu as pltpu
from jax.sharding import PartitionSpec as P

MESH = pl.DeviceIdType.MESH
VLIMIT = 48 * 1024 * 1024
F32 = jnp.float32
BF16 = jnp.bfloat16
CHUNK = 512


def run_chain(x, params):
    members, lanes = x.shape
    lane = lax.broadcasted_iota(jnp.int32, (1, lanes), 1)
    mean = jnp.mean(x, axis=0, keepdims=True)
    a = x - mean
    row, col, rad = params[0:1, :], params[1:2, :], params[2:3, :]
    inv_rad2 = 1.0 / (rad * rad)
    obs, err = params[3:4, :], params[4:5, :]
    for k in range(lanes):
        def pick(v, k=k):
            return jnp.broadcast_to(v[:, k:k + 1], v.shape)
        dr, dc = row - pick(row), col - pick(col)
        taper = jnp.square(jnp.maximum(1.0 - (dr * dr + dc * dc) * pick(inv_rad2), 0.0))
        taper = jnp.where(lane > k, taper, 0.0) * (1.0 / (members - 1))
        r, o = pick(err), pick(obs)
        ak = pick(a)
        mk = pick(mean)
        cov = jnp.sum(a * ak, axis=0, keepdims=True)
        s2 = jnp.sum(ak * ak, axis=0, keepdims=True) * (1.0 / (members - 1)) + 1e-05
        inv = 1.0 / (s2 + r)
        shift = s2 * (o - mk) * inv
        beta = jnp.sqrt(r * inv) - 1.0
        w = taper * cov / s2
        a = a + (w * beta) * ak
        mean = mean + w * shift
    return a, mean


def stencil_terms(cr, cc, kk):
    pr, mr = jnp.maximum(cr, 0.0), jnp.minimum(cr, 0.0)
    pc, mc = jnp.maximum(cc, 0.0), jnp.minimum(cc, 0.0)
    return 1.0 - pr + mr - pc + mc - 4.0 * kk, pr + kk, kk - mr, pc + kk, kk - mc


def front_kernel(nx, ny, owner, trow, tcol, order, radius, obs, err, state_in, cr_ref, cc_ref, k_ref,
                 out, anomalies_out, means_out, params_out,
                 raw, once, two, coef, coef_top, coef_bottom, edge_once, edge,
                 row_pack, col_pack, row_coef, col_coef, corner_coef, row_in, col_in, corner_in, acc, recv,
                 load_sem, cs, cr_sem, hs, hr, ss, rs):
    size, cols = state_in.shape
    members = size // 8
    blocks = cols // 128
    count = trow.shape[1]
    wide = cols + 256
    gx = lax.axis_index("gx")
    gy = lax.axis_index("gy")
    loads = [
        pltpu.make_async_copy(state_in.at[:, pl.ds(j * 128, 128)], raw.at[j + 1], load_sem.at[j])
        for j in range(blocks)
    ]
    for load in loads:
        load.start()
    steps = [(-1, 0), (1, 0), (0, -1), (0, 1), (-1, -1), (-1, 1), (1, -1), (1, 1)]
    opposite = [1, 0, 3, 2, 7, 6, 5, 4]
    low_x, high_x, low_y, high_y = gx > 0, gx < nx - 1, gy > 0, gy < ny - 1
    has = [low_x, high_x, low_y, high_y, low_x & low_y, low_x & high_y, high_x & low_y, high_x & high_y]
    peer = [(jnp.clip(gx + dx, 0, nx - 1), jnp.clip(gy + dy, 0, ny - 1)) for dx, dy in steps]
    partners = []
    bit = 1
    while bit < ny:
        partners.append((gx, gy + bit - 2 * bit * ((gy // bit) % 2)))
        bit *= 2
    bit = 1
    while bit < nx:
        partners.append((gx + bit - 2 * bit * ((gx // bit) % 2), gy))
        bit *= 2
    row_coef[...] = jnp.zeros(row_coef.shape, F32)
    col_coef[...] = jnp.zeros(col_coef.shape, F32)
    corner_coef[...] = jnp.zeros(corner_coef.shape, F32)
    barrier = pltpu.get_barrier_semaphore()
    for d in range(8):
        @pl.when(has[d])
        def _(d=d):
            pl.semaphore_signal(barrier, inc=1, device_id=peer[d], device_id_type=MESH)
    for p in partners:
        pl.semaphore_signal(barrier, inc=1, device_id=p, device_id_type=MESH)

    cr, cc, kk = cr_ref[...], cc_ref[...], k_ref[...]
    zero2 = jnp.zeros((2, cols), F32)
    row_pack[0] = jnp.concatenate(
        [cr[0:1], cc[0:1], kk[0:1], cr[1:2], cc[1:2], kk[1:2], zero2], axis=0)
    row_pack[1] = jnp.concatenate(
        [cr[7:8], cc[7:8], kk[7:8], cr[6:7], cc[6:7], kk[6:7], zero2], axis=0)
    for d in range(2):
        lanes = slice(0, 128) if d == 0 else slice(cols - 128, cols)
        col_pack[d] = jnp.concatenate([cr[:, lanes], cc[:, lanes], kk[:, lanes]], axis=0)
    pl.semaphore_wait(barrier, sum(h.astype(jnp.int32) for h in has) + len(partners))

    def small(d):
        q = opposite[d]
        if d < 2:
            source, target = row_pack.at[d], row_coef.at[q]
        elif d < 4:
            source, target = col_pack.at[d - 2], col_coef.at[q - 2]
        else:
            side, end = (d - 4) // 2, (d - 4) % 2
            source = row_pack.at[side, :, pl.ds(0 if end == 0 else cols - 128, 128)]
            target = corner_coef.at[q - 4]
        return pltpu.make_async_remote_copy(
            source, target, cs.at[d], cr_sem.at[q], device_id=peer[d], device_id_type=MESH)

    def bulk(d):
        q = opposite[d]
        if d < 2:
            source, target = edge.at[d, :, pl.ds(1, blocks)], row_in.at[q]
        elif d < 4:
            source, target = two.at[0 if d == 2 else blocks + 1], col_in.at[q - 2]
        else:
            side, end = (d - 4) // 2, (d - 4) % 2
            source, target = edge.at[side, 0, 0 if end == 0 else blocks + 1], corner_in.at[q - 4]
        return pltpu.make_async_remote_copy(
            source, target, hs.at[d], hr.at[q], device_id=peer[d], device_id_type=MESH)

    def each(action):
        for d in (4, 5, 6, 7, 2, 3, 0, 1):
            @pl.when(has[d])
            def _(d=d):
                action(d)

    each(lambda d: small(d).start())
    raw[0] = jnp.zeros((size, 128), F32)
    raw[blocks + 1] = jnp.zeros((size, 128), F32)
    each(lambda d: small(d).wait_send())
    for d in range(8):
        @pl.when(has[d])
        def _(d=d):
            small(opposite[d]).wait_recv()

    def widen(i, v):
        return jnp.concatenate([col_coef[0, i * 8:i * 8 + 8, :], v, col_coef[1, i * 8:i * 8 + 8, :]], axis=1)

    for i, term in enumerate(stencil_terms(widen(0, cr), widen(1, cc), widen(2, kk))):
        coef[i] = term
    for side, target in ((0, coef_top), (1, coef_bottom)):
        rows = jnp.concatenate(
            [corner_coef[2 * side], row_coef[side], corner_coef[2 * side + 1]], axis=1)
        near = stencil_terms(rows[0:1], rows[1:2], rows[2:3])
        far = stencil_terms(rows[3:4], rows[4:5], rows[5:6])
        for i in range(5):
            target[i:i + 1, :] = near[i]
        target[5:6, :] = far[2] if side == 0 else far[1]
    for load in loads:
        load.wait()

    def block(ref, j, i):
        return ref[i:i + 1, j * 128:(j + 1) * 128]

    for j in range(blocks + 2):
        edge_once[0, j] = block(coef_top, j, 2) * raw[j, pl.ds(0, members, stride=8), :]
        edge_once[1, j] = block(coef_bottom, j, 1) * raw[j, pl.ds(7, members, stride=8), :]
    sub = lax.broadcasted_iota(jnp.int32, (8, wide), 0)
    top, bottom = sub == 0, sub == 7

    def substep(source, target, edges):
        def member(e, carry):
            rows = pl.ds(pl.multiple_of(e * 8, 8), 8)
            center = jnp.concatenate([source[j, rows, :] for j in range(blocks + 2)], axis=1)
            left = pltpu.roll(center, 1, 1)
            right = pltpu.roll(center, wide - 1, 1)
            if edges:
                above = jnp.concatenate([edge_once[0, j, pl.ds(e, 1), :] for j in range(blocks + 2)], axis=1)
                below = jnp.concatenate([edge_once[1, j, pl.ds(e, 1), :] for j in range(blocks + 2)], axis=1)
            else:
                above = below = 0.0
            up = jnp.where(top, above, pltpu.roll(center, 1, 0))
            down = jnp.where(bottom, below, pltpu.roll(center, 7, 0))
            new = coef[0] * center + coef[1] * up + coef[2] * down + coef[3] * left + coef[4] * right
            for j in range(blocks + 2):
                target[j, rows, :] = new[:, j * 128:(j + 1) * 128]
            return carry

        lax.fori_loop(0, members, member, 0)

    substep(raw, once, False)
    for side, terms, toward, r in ((0, coef_top, 2, 0), (1, coef_bottom, 1, 7)):
        for j in range(blocks + 2):
            edge[side, 0, j] = block(terms, j, toward) * once[j, pl.ds(r, members, stride=8), :]

        def group(i, carry, side=side, terms=terms):
            rows = pl.ds(pl.multiple_of(i * 8, 8), 8)
            e = jnp.concatenate([edge_once[side, j, rows, :] for j in range(blocks + 2)], axis=1)
            near = terms[0:1, :] * e + terms[3:4, :] * pltpu.roll(e, 1, 1) + terms[4:5, :] * pltpu.roll(e, wide - 1, 1)
            far = terms[5:6, :] * e
            for j in range(blocks + 2):
                lanes = slice(j * 128, (j + 1) * 128)
                edge[side, 0, j, rows, :] = edge[side, 0, j, rows, :] + near[:, lanes]
                edge[side, 1, j, rows, :] = far[:, lanes]
            return carry

        lax.fori_loop(0, members // 8, group, 0)
    substep(once, two, True)
    each(lambda d: bulk(d).start())

    lanes_m = lax.broadcasted_iota(jnp.int32, (members, 128), 1)
    sub8 = lax.broadcasted_iota(jnp.int32, (8, 128), 0)
    lane8 = lax.broadcasted_iota(jnp.int32, (8, 128), 1)
    unroll = 16
    values = jnp.zeros((members, 128), F32)
    par = jnp.zeros((8, 128), F32)
    for b in range(2):
        own = owner[b]
        base_row = lax.div(own, jnp.int32(ny)) * 8
        base_col = lax.rem(own, jnp.int32(ny)) * cols

        def body(blk, carry, b=b, base_row=base_row, base_col=base_col):
            values, par = carry
            for i in range(unroll):
                at = b * count + blk * unroll + i
                k = order[b, blk * unroll + i]
                grow = base_row + trow[b, k]
                gcol = base_col + tcol[b, k]
                r = grow - gx * 8
                c = gcol - gy * cols + 128
                inside = (r >= -2) & (r <= 9) & (c >= 126) & (c <= cols + 129)
                c = jnp.clip(c, 0, wide - 1)
                place = lax.div(c, jnp.int32(128))
                inner = c - place * 128
                main = (r >= 0) & (r <= 7)
                side = jnp.where(r < 0, 0, 1)
                depth = jnp.clip(jnp.where(r < 0, -1 - r, r - 8), 0, 1)
                x = two[place, pl.ds(jnp.clip(r, 0, 7), members, stride=8), :]
                y = edge[side, depth, place]
                x = jnp.where(main, x, y)
                x = pltpu.roll(x, lax.rem(at - inner + 128, jnp.int32(128)), 1)
                values = jnp.where(lanes_m == jnp.where(inside, at, -1), x, values)
                new = jnp.where(
                    sub8 == 0, grow.astype(F32),
                    jnp.where(sub8 == 1, gcol.astype(F32),
                              jnp.where(sub8 == 2, radius[b, k].astype(F32),
                                        jnp.where(sub8 == 3, obs[b, k], err[b, k]))))
                par = jnp.where(lane8 == at, new, par)
            return values, par

        values, par = lax.fori_loop(0, count // unroll, body, (values, par))
    params_out[...] = par

    acc[0] = values
    copies = []
    for s, p in enumerate(partners):
        copy = pltpu.make_async_remote_copy(
            acc.at[s], recv.at[s], ss.at[s], rs.at[s], device_id=p, device_id_type=MESH)
        copy.start()
        copies.append(copy)
        copy.wait_recv()
        acc[s + 1] = acc[s] + recv[s]
    a, mean = run_chain(acc[len(partners)], par)
    anomalies_out[...] = a
    means_out[...] = jnp.broadcast_to(mean, (8, 128))

    for j in range(blocks):
        out[j] = two[j + 1]
    for d in range(8):
        @pl.when(has[d])
        def _(d=d):
            bulk(opposite[d]).wait_recv()
            if d < 2:
                rows = (0, 1) if d == 0 else (7, 6)
                for depth in range(2):
                    for j in range(blocks):
                        where = (j, pl.ds(rows[depth], members, stride=8), slice(None))
                        out[where] = out[where] + row_in[d, depth, j]
            elif d < 4:
                j = 0 if d == 2 else blocks - 1
                out[j] = out[j] + col_in[d - 2]
            else:
                where = (0 if d % 2 == 0 else blocks - 1,
                         pl.ds(0 if d < 6 else 7, members, stride=8), slice(None))
                out[where] = out[where] + corner_in[d - 4]
    each(lambda d: bulk(d).wait_send())
    for copy in copies:
        copy.wait_send()


def front(nx, ny, smalls, state, cr, cc, kk):
    size, cols = state.shape
    members = size // 8
    blocks = cols // 128
    wide = cols + 256
    stages = (nx.bit_length() - 1) + (ny.bit_length() - 1)
    vmem = pl.BlockSpec(memory_space=pltpu.VMEM)
    smem = pl.BlockSpec(memory_space=pltpu.SMEM)
    dma = pltpu.SemaphoreType.DMA
    return pl.pallas_call(
        functools.partial(front_kernel, nx, ny),
        out_shape=(
            jax.ShapeDtypeStruct((blocks, size, 128), F32),
            jax.ShapeDtypeStruct((members, 128), F32),
            jax.ShapeDtypeStruct((8, 128), F32),
            jax.ShapeDtypeStruct((8, 128), F32),
        ),
        in_specs=[smem] * 7 + [pl.BlockSpec(memory_space=pl.ANY)] + [vmem] * 3,
        out_specs=(vmem,) * 4,
        scratch_shapes=[
            pltpu.VMEM((blocks + 2, size, 128), F32),
            pltpu.VMEM((blocks + 2, size, 128), F32),
            pltpu.VMEM((blocks + 2, size, 128), F32),
            pltpu.VMEM((5, 8, wide), F32),
            pltpu.VMEM((8, wide), F32),
            pltpu.VMEM((8, wide), F32),
            pltpu.VMEM((2, blocks + 2, members, 128), F32),
            pltpu.VMEM((2, 2, blocks + 2, members, 128), F32),
            pltpu.VMEM((2, 8, cols), F32),
            pltpu.VMEM((2, 24, 128), F32),
            pltpu.VMEM((2, 8, cols), F32),
            pltpu.VMEM((2, 24, 128), F32),
            pltpu.VMEM((4, 8, 128), F32),
            pltpu.VMEM((2, 2, blocks, members, 128), F32),
            pltpu.VMEM((2, size, 128), F32),
            pltpu.VMEM((4, members, 128), F32),
            pltpu.VMEM((stages + 1, members, 128), F32),
            pltpu.VMEM((stages, members, 128), F32),
            dma((blocks,)), dma((8,)), dma((8,)), dma((8,)), dma((8,)), dma((stages,)), dma((stages,)),
        ],
        compiler_params=pltpu.CompilerParams(
            collective_id=0, has_side_effects=True, vmem_limit_bytes=VLIMIT),
        name="front",
    )(*smalls, state, cr, cc, kk)


def split(x):
    hi = x.astype(BF16)
    return hi, (x - hi.astype(F32)).astype(BF16)


def apply_kernel(adv, anomalies, means, params, final, out, coupling, weights, tapers, lhs1, lhs2):
    members, lanes = anomalies.shape
    blocks = adv.shape[0]
    cols = blocks * 128
    count = lanes // 2
    width = CHUNK // 128
    row_base = lax.axis_index("gx") * 8
    col_base = lax.axis_index("gy") * cols
    a = anomalies[...]
    mean = means[0:1, :]
    col, rad = params[1:2, :], params[2:3, :]
    obs, err = params[3:4, :], params[4:5, :]
    s2 = jnp.sum(a * a, axis=0, keepdims=True) * (1.0 / (members - 1)) + 1e-05
    inv = 1.0 / (s2 + err)
    shift = s2 * (obs - mean) * inv
    beta = jnp.sqrt(err * inv) - 1.0
    delta = beta * a
    pad = jnp.zeros((lanes - members, lanes), F32)
    at = jnp.concatenate([a, pad], axis=0).T
    g = jnp.dot(at, jnp.concatenate([delta, pad], axis=0), precision=lax.Precision.HIGHEST,
                preferred_element_type=F32)
    for s in range(lanes):
        b = s // count
        coupling[s] = jnp.broadcast_to(g[b * count:(b + 1) * count, s:s + 1], (count, lanes))
    ahi, alo = split(a)
    ahi, alo = ahi.astype(F32), alo.astype(F32)
    stacked = jnp.concatenate([ahi, ahi, alo, jnp.zeros_like(alo)], axis=0)
    lhs1[...] = stacked.T.astype(BF16)
    dd = delta + shift
    dhi, dlo = split(dd)
    dhi, dlo = dhi.astype(F32), dlo.astype(F32)
    for b in range(2):
        part = slice(b * count, (b + 1) * count)
        lhs2[b] = jnp.concatenate(
            [dhi[:, part], dhi[:, part], dlo[:, part], jnp.zeros((members, count), F32)], axis=1).astype(BF16)
    pt = jnp.concatenate(
        [params[0:3, :], 1.0 / (s2 * (members - 1)), jnp.zeros((lanes - 4, lanes), F32)], axis=0).T
    lane = lax.broadcasted_iota(jnp.int32, (1, lanes), 1)
    big = 1e9
    low, high = [], []
    for b in range(2):
        inside = (lane >= b * count) & (lane < (b + 1) * count)
        low.append(jnp.min(jnp.where(inside, col - rad, big)))
        high.append(jnp.max(jnp.where(inside, col + rad, -big)))
    cells = lax.broadcasted_iota(jnp.int32, (count, CHUNK), 1)
    chunks = cols // CHUNK

    def step(number, carry):
        r = number // chunks
        chunk = number % chunks
        start = pl.multiple_of(chunk * CHUNK, CHUNK)
        places = [(chunk * width + j, pl.ds(r, members, stride=8)) for j in range(width)]
        for place in places:
            out[place] = adv[place]
        first = (col_base + start).astype(F32)
        grow = (row_base + r).astype(F32)
        for b in range(2):
            part = slice(b * count, (b + 1) * count)

            @pl.when((first + (CHUNK - 1.0) > low[b]) & (first < high[b]))
            def _(b=b, part=part):
                x = jnp.concatenate([out[place] for place in places], axis=1)
                dr = pt[part, 0:1] - grow
                dc = (cells + (col_base + start)).astype(F32) - pt[part, 1:2]
                inv2 = 1.0 / (pt[part, 2:3] * pt[part, 2:3])
                t = jnp.maximum(1.0 - (dr * dr + dc * dc) * inv2, 0.0)
                tapers[...] = t * t * pt[part, 3:4]
                xhi, xlo = split(x)
                carried = jnp.dot(
                    lhs1[part, :], jnp.concatenate([xhi, xlo, xhi, jnp.zeros_like(xhi)], axis=0),
                    preferred_element_type=F32)
                groups = [carried[i * 8:(i + 1) * 8, :] for i in range(count // 8)]
                for k in range(count):
                    gi, si = k // 8, k % 8
                    w = groups[gi][si:si + 1, :] * tapers[k:k + 1, :]
                    weights[k:k + 1, :] = w
                    first_group = gi if si < 7 else gi + 1
                    for gj in range(first_group, count // 8):
                        c = coupling[b * count + k, gj * 8:(gj + 1) * 8, :]
                        c = jnp.concatenate([c] * (CHUNK // 128), axis=1)
                        groups[gj] = groups[gj] + c * w
                whi, wlo = split(weights[...])
                x = x + jnp.dot(
                    lhs2[b], jnp.concatenate([whi, wlo, whi, jnp.zeros_like(whi)], axis=0),
                    preferred_element_type=F32)
                for j, place in enumerate(places):
                    out[place] = x[:, j * 128:(j + 1) * 128]
        return carry

    lax.fori_loop(0, 8 * chunks, step, 0)
    for j in range(blocks):
        final[:, j * 128:(j + 1) * 128] = out[j]


def apply(adv, anomalies, means, params):
    members, lanes = anomalies.shape
    count = lanes // 2
    vmem = pl.BlockSpec(memory_space=pltpu.VMEM)
    return pl.pallas_call(
        apply_kernel,
        out_shape=jax.ShapeDtypeStruct((adv.shape[1], adv.shape[0] * 128), F32),
        in_specs=[vmem] * 4,
        out_specs=vmem,
        scratch_shapes=[
            pltpu.VMEM(adv.shape, F32),
            pltpu.VMEM((lanes, count, lanes), F32),
            pltpu.VMEM((count, CHUNK), F32),
            pltpu.VMEM((count, CHUNK), F32),
            pltpu.VMEM((lanes, 256), BF16),
            pltpu.VMEM((2, members, 256), BF16),
        ],
        compiler_params=pltpu.CompilerParams(vmem_limit_bytes=VLIMIT),
        name="apply",
    )(adv, anomalies, means, params)


def solution(mesh):
    nx, ny = mesh.shape["gx"], mesh.shape["gy"]

    def local(state, cr, cc, kk, owner, trow, tcol, order, radius, obs, err):
        members, rows, cols = state.shape
        smalls = (owner, trow, tcol, order, radius, obs, err)
        adv, anomalies, means, params = front(nx, ny, smalls, state.reshape(members * rows, cols), cr, cc, kk)
        out = apply(adv, anomalies, means, params)
        return out.reshape(members, rows, cols)

    split_spec = P(None, "gx", "gy")
    cell = P("gx", "gy")
    return jax.shard_map(
        local, mesh=mesh, in_specs=(split_spec,) + (cell,) * 3 + (P(),) * 7, out_specs=split_spec, check_vma=False)
```

```python
import functools
import jax
import jax.numpy as jnp
from jax import lax
from jax.experimental import pallas as pl
from jax.experimental.pallas import tpu as pltpu
from jax.sharding import PartitionSpec as P

MESH = pl.DeviceIdType.MESH
VLIMIT = 63 * 1024 * 1024
F32 = jnp.float32
BF16 = jnp.bfloat16
CHUNK = 512


def run_chain(x, params):
    members, lanes = x.shape
    lane = lax.broadcasted_iota(jnp.int32, (1, lanes), 1)
    mean = jnp.mean(x, axis=0, keepdims=True)
    a = x - mean
    row, col, rad = params[0:1, :], params[1:2, :], params[2:3, :]
    inv_rad2 = 1.0 / (rad * rad)
    obs, err = params[3:4, :], params[4:5, :]
    for k in range(lanes):
        def pick(v, k=k):
            return jnp.broadcast_to(v[:, k:k + 1], v.shape)
        dr, dc = row - pick(row), col - pick(col)
        taper = jnp.square(jnp.maximum(1.0 - (dr * dr + dc * dc) * pick(inv_rad2), 0.0))
        taper = jnp.where(lane > k, taper, 0.0) * (1.0 / (members - 1))
        r, o = pick(err), pick(obs)
        ak = pick(a)
        mk = pick(mean)
        cov = jnp.sum(a * ak, axis=0, keepdims=True)
        s2 = jnp.sum(ak * ak, axis=0, keepdims=True) * (1.0 / (members - 1)) + 1e-05
        inv = 1.0 / (s2 + r)
        shift = s2 * (o - mk) * inv
        beta = jnp.sqrt(r * inv) - 1.0
        w = taper * cov / s2
        a = a + (w * beta) * ak
        mean = mean + w * shift
    return a, mean


def stencil_terms(cr, cc, kk):
    pr, mr = jnp.maximum(cr, 0.0), jnp.minimum(cr, 0.0)
    pc, mc = jnp.maximum(cc, 0.0), jnp.minimum(cc, 0.0)
    return 1.0 - pr + mr - pc + mc - 4.0 * kk, pr + kk, kk - mr, pc + kk, kk - mc


def front_kernel(nx, ny, owner_in, trow_in, tcol_in, order_in, radius_in, obs_in, err_in, state_in, cr_in, cc_in, k_in,
                 out, anomalies_out, means_out, params_out,
                 raw, once, two, coef, coef_top, coef_bottom, edge_once, edge,
                 row_pack, col_pack, row_coef, col_coef, corner_coef, row_in, col_in, corner_in, acc, recv,
                 owner, trow, tcol, order, radius, obs, err, cr_ref, cc_ref, k_ref,
                 load_sem, small_sem, cs, cr_sem, hs, hr, ss, rs):
    size, cols = state_in.shape
    members = size // 8
    blocks = cols // 128
    count = trow.shape[1]
    wide = cols + 256
    gx = lax.axis_index("gx")
    gy = lax.axis_index("gy")
    loads = [
        pltpu.make_async_copy(state_in.at[:, pl.ds(j * 128, 128)], raw.at[j + 1], load_sem.at[j])
        for j in range(blocks)
    ]
    field_loads = [
        pltpu.make_async_copy(source, target, small_sem.at[i])
        for i, (source, target) in enumerate(((cr_in, cr_ref), (cc_in, cc_ref), (k_in, k_ref)))
    ]
    table_loads = [
        pltpu.make_async_copy(source, target, small_sem.at[3 + i])
        for i, (source, target) in enumerate((
            (owner_in, owner), (trow_in, trow), (tcol_in, tcol), (order_in, order), (radius_in, radius),
            (obs_in, obs), (err_in, err)))
    ]
    for load in field_loads + loads + table_loads:
        load.start()
    steps = [(-1, 0), (1, 0), (0, -1), (0, 1), (-1, -1), (-1, 1), (1, -1), (1, 1)]
    opposite = [1, 0, 3, 2, 7, 6, 5, 4]
    low_x, high_x, low_y, high_y = gx > 0, gx < nx - 1, gy > 0, gy < ny - 1
    has = [low_x, high_x, low_y, high_y, low_x & low_y, low_x & high_y, high_x & low_y, high_x & high_y]
    peer = [(jnp.clip(gx + dx, 0, nx - 1), jnp.clip(gy + dy, 0, ny - 1)) for dx, dy in steps]
    partners = []
    bit = 1
    while bit < ny:
        partners.append((gx, gy + bit - 2 * bit * ((gy // bit) % 2)))
        bit *= 2
    bit = 1
    while bit < nx:
        partners.append((gx + bit - 2 * bit * ((gx // bit) % 2), gy))
        bit *= 2
    row_coef[...] = jnp.zeros(row_coef.shape, F32)
    col_coef[...] = jnp.zeros(col_coef.shape, F32)
    corner_coef[...] = jnp.zeros(corner_coef.shape, F32)
    barrier = pltpu.get_barrier_semaphore()
    for d in range(8):
        @pl.when(has[d])
        def _(d=d):
            pl.semaphore_signal(barrier, inc=1, device_id=peer[d], device_id_type=MESH)
    for p in partners:
        pl.semaphore_signal(barrier, inc=1, device_id=p, device_id_type=MESH)

    for load in field_loads:
        load.wait()
    cr, cc, kk = cr_ref[...], cc_ref[...], k_ref[...]
    zero2 = jnp.zeros((2, cols), F32)
    row_pack[0] = jnp.concatenate(
        [cr[0:1], cc[0:1], kk[0:1], cr[1:2], cc[1:2], kk[1:2], zero2], axis=0)
    row_pack[1] = jnp.concatenate(
        [cr[7:8], cc[7:8], kk[7:8], cr[6:7], cc[6:7], kk[6:7], zero2], axis=0)
    for d in range(2):
        lanes = slice(0, 128) if d == 0 else slice(cols - 128, cols)
        col_pack[d] = jnp.concatenate([cr[:, lanes], cc[:, lanes], kk[:, lanes]], axis=0)
    pl.semaphore_wait(barrier, sum(h.astype(jnp.int32) for h in has) + len(partners))

    def small(d):
        q = opposite[d]
        if d < 2:
            source, target = row_pack.at[d], row_coef.at[q]
        elif d < 4:
            source, target = col_pack.at[d - 2], col_coef.at[q - 2]
        else:
            side, end = (d - 4) // 2, (d - 4) % 2
            source = row_pack.at[side, :, pl.ds(0 if end == 0 else cols - 128, 128)]
            target = corner_coef.at[q - 4]
        return pltpu.make_async_remote_copy(
            source, target, cs.at[d], cr_sem.at[q], device_id=peer[d], device_id_type=MESH)

    def bulk(d):
        q = opposite[d]
        if d < 2:
            source, target = edge.at[d, 0, pl.ds(1, blocks)], row_in.at[q, 0]
        elif d < 4:
            source, target = two.at[0 if d == 2 else blocks + 1], col_in.at[q - 2]
        else:
            side, end = (d - 4) // 2, (d - 4) % 2
            source, target = edge.at[side, 0, 0 if end == 0 else blocks + 1], corner_in.at[q - 4]
        return pltpu.make_async_remote_copy(
            source, target, hs.at[d], hr.at[q], device_id=peer[d], device_id_type=MESH)

    def far_rows(d):
        q = opposite[d]
        return pltpu.make_async_remote_copy(
            edge.at[d, 1, pl.ds(1, blocks)], row_in.at[q, 1], hs.at[8 + d], hr.at[8 + q],
            device_id=peer[d], device_id_type=MESH)

    def each(action, which=(4, 5, 6, 7, 2, 3, 0, 1)):
        for d in which:
            @pl.when(has[d])
            def _(d=d):
                action(d)

    each(lambda d: small(d).start())
    raw[0] = jnp.zeros((size, 128), F32)
    raw[blocks + 1] = jnp.zeros((size, 128), F32)
    each(lambda d: small(d).wait_send())
    for d in range(8):
        @pl.when(has[d])
        def _(d=d):
            small(opposite[d]).wait_recv()

    def widen(i, v):
        return jnp.concatenate([col_coef[0, i * 8:i * 8 + 8, :], v, col_coef[1, i * 8:i * 8 + 8, :]], axis=1)

    for i, term in enumerate(stencil_terms(widen(0, cr), widen(1, cc), widen(2, kk))):
        coef[i] = term
    for side, target in ((0, coef_top), (1, coef_bottom)):
        rows = jnp.concatenate(
            [corner_coef[2 * side], row_coef[side], corner_coef[2 * side + 1]], axis=1)
        near = stencil_terms(rows[0:1], rows[1:2], rows[2:3])
        far = stencil_terms(rows[3:4], rows[4:5], rows[5:6])
        for i in range(5):
            target[i:i + 1, :] = near[i]
        target[5:6, :] = far[2] if side == 0 else far[1]
    for load in loads:
        load.wait()

    def block(ref, j, i):
        return ref[i:i + 1, j * 128:(j + 1) * 128]

    for j in range(blocks + 2):
        edge_once[0, j] = block(coef_top, j, 2) * raw[j, pl.ds(0, members, stride=8), :]
        edge_once[1, j] = block(coef_bottom, j, 1) * raw[j, pl.ds(7, members, stride=8), :]
        edge[0, 1, j] = block(coef_top, j, 5) * edge_once[0, j]
        edge[1, 1, j] = block(coef_bottom, j, 5) * edge_once[1, j]
    each(lambda d: far_rows(d).start(), (0, 1))
    sub = lax.broadcasted_iota(jnp.int32, (8, wide), 0)
    top, bottom = sub == 0, sub == 7

    def substep(source, target, edges):
        def member(e, carry):
            rows = pl.ds(pl.multiple_of(e * 8, 8), 8)
            center = jnp.concatenate([source[j, rows, :] for j in range(blocks + 2)], axis=1)
            left = pltpu.roll(center, 1, 1)
            right = pltpu.roll(center, wide - 1, 1)
            if edges:
                above = jnp.concatenate([edge_once[0, j, pl.ds(e, 1), :] for j in range(blocks + 2)], axis=1)
                below = jnp.concatenate([edge_once[1, j, pl.ds(e, 1), :] for j in range(blocks + 2)], axis=1)
            else:
                above = below = 0.0
            up = jnp.where(top, above, pltpu.roll(center, 1, 0))
            down = jnp.where(bottom, below, pltpu.roll(center, 7, 0))
            new = coef[0] * center + coef[1] * up + coef[2] * down + coef[3] * left + coef[4] * right
            for j in range(blocks + 2):
                target[j, rows, :] = new[:, j * 128:(j + 1) * 128]
            return carry

        lax.fori_loop(0, members, member, 0)

    substep(raw, once, False)
    for side, terms, toward, r in ((0, coef_top, 2, 0), (1, coef_bottom, 1, 7)):
        for j in range(blocks + 2):
            edge[side, 0, j] = block(terms, j, toward) * once[j, pl.ds(r, members, stride=8), :]

        def group(i, carry, side=side, terms=terms):
            rows = pl.ds(pl.multiple_of(i * 8, 8), 8)
            e = jnp.concatenate([edge_once[side, j, rows, :] for j in range(blocks + 2)], axis=1)
            near = terms[0:1, :] * e + terms[3:4, :] * pltpu.roll(e, 1, 1) + terms[4:5, :] * pltpu.roll(e, wide - 1, 1)
            for j in range(blocks + 2):
                lanes = slice(j * 128, (j + 1) * 128)
                edge[side, 0, j, rows, :] = edge[side, 0, j, rows, :] + near[:, lanes]
            return carry

        lax.fori_loop(0, members // 8, group, 0)
    substep(once, two, True)
    each(lambda d: bulk(d).start(), (2, 3))
    for load in table_loads:
        load.wait()

    lanes_m = lax.broadcasted_iota(jnp.int32, (members, 128), 1)
    sub8 = lax.broadcasted_iota(jnp.int32, (8, 128), 0)
    lane8 = lax.broadcasted_iota(jnp.int32, (8, 128), 1)
    unroll = 16
    values = jnp.zeros((members, 128), F32)
    par = jnp.zeros((8, 128), F32)
    for b in range(2):
        own = owner[b]
        base_row = lax.div(own, jnp.int32(ny)) * 8
        base_col = lax.rem(own, jnp.int32(ny)) * cols

        def body(blk, carry, b=b, base_row=base_row, base_col=base_col):
            values, par = carry
            for i in range(unroll):
                at = b * count + blk * unroll + i
                k = order[b, blk * unroll + i]
                grow = base_row + trow[b, k]
                gcol = base_col + tcol[b, k]
                r = grow - gx * 8
                c = gcol - gy * cols + 128
                inside = (r >= -2) & (r <= 9) & (c >= 126) & (c <= cols + 129)
                c = jnp.clip(c, 0, wide - 1)
                place = lax.div(c, jnp.int32(128))
                inner = c - place * 128
                main = (r >= 0) & (r <= 7)
                side = jnp.where(r < 0, 0, 1)
                depth = jnp.clip(jnp.where(r < 0, -1 - r, r - 8), 0, 1)
                x = two[place, pl.ds(jnp.clip(r, 0, 7), members, stride=8), :]
                y = edge[side, depth, place]
                x = jnp.where(main, x, y)
                x = pltpu.roll(x, lax.rem(at - inner + 128, jnp.int32(128)), 1)
                values = jnp.where(lanes_m == jnp.where(inside, at, -1), x, values)
                new = jnp.where(
                    sub8 == 0, grow.astype(F32),
                    jnp.where(sub8 == 1, gcol.astype(F32),
                              jnp.where(sub8 == 2, radius[b, k].astype(F32),
                                        jnp.where(sub8 == 3, obs[b, k], err[b, k]))))
                par = jnp.where(lane8 == at, new, par)
            return values, par

        values, par = lax.fori_loop(0, count // unroll, body, (values, par))
    params_out[...] = par

    acc[0] = values
    copies = []
    for s, p in enumerate(partners):
        copy = pltpu.make_async_remote_copy(
            acc.at[s], recv.at[s], ss.at[s], rs.at[s], device_id=p, device_id_type=MESH)
        copy.start()
        copies.append(copy)
        copy.wait_recv()
        acc[s + 1] = acc[s] + recv[s]
    each(lambda d: bulk(d).start(), (0, 1, 4, 5, 6, 7))
    a, mean = run_chain(acc[len(partners)], par)
    anomalies_out[...] = a
    means_out[...] = jnp.broadcast_to(mean, (8, 128))

    for j in range(blocks):
        out[j] = two[j + 1]
    for d in range(8):
        @pl.when(has[d])
        def _(d=d):
            bulk(opposite[d]).wait_recv()
            if d < 2:
                far_rows(opposite[d]).wait_recv()
                rows = (0, 1) if d == 0 else (7, 6)
                for depth in range(2):
                    for j in range(blocks):
                        where = (j, pl.ds(rows[depth], members, stride=8), slice(None))
                        out[where] = out[where] + row_in[d, depth, j]
            elif d < 4:
                j = 0 if d == 2 else blocks - 1
                out[j] = out[j] + col_in[d - 2]
            else:
                where = (0 if d % 2 == 0 else blocks - 1,
                         pl.ds(0 if d < 6 else 7, members, stride=8), slice(None))
                out[where] = out[where] + corner_in[d - 4]
    each(lambda d: bulk(d).wait_send())
    each(lambda d: far_rows(d).wait_send(), (0, 1))
    for copy in copies:
        copy.wait_send()


def front(nx, ny, smalls, state, cr, cc, kk):
    size, cols = state.shape
    members = size // 8
    blocks = cols // 128
    wide = cols + 256
    stages = (nx.bit_length() - 1) + (ny.bit_length() - 1)
    vmem = pl.BlockSpec(memory_space=pltpu.VMEM)
    dma = pltpu.SemaphoreType.DMA
    return pl.pallas_call(
        functools.partial(front_kernel, nx, ny),
        out_shape=(
            jax.ShapeDtypeStruct((blocks, size, 128), F32),
            jax.ShapeDtypeStruct((members, 128), F32),
            jax.ShapeDtypeStruct((8, 128), F32),
            jax.ShapeDtypeStruct((8, 128), F32),
        ),
        in_specs=[pl.BlockSpec(memory_space=pltpu.HBM)] * 11,
        out_specs=(vmem,) * 4,
        scratch_shapes=[
            pltpu.VMEM((blocks + 2, size, 128), F32),
            pltpu.VMEM((blocks + 2, size, 128), F32),
            pltpu.VMEM((blocks + 2, size, 128), F32),
            pltpu.VMEM((5, 8, wide), F32),
            pltpu.VMEM((8, wide), F32),
            pltpu.VMEM((8, wide), F32),
            pltpu.VMEM((2, blocks + 2, members, 128), F32),
            pltpu.VMEM((2, 2, blocks + 2, members, 128), F32),
            pltpu.VMEM((2, 8, cols), F32),
            pltpu.VMEM((2, 24, 128), F32),
            pltpu.VMEM((2, 8, cols), F32),
            pltpu.VMEM((2, 24, 128), F32),
            pltpu.VMEM((4, 8, 128), F32),
            pltpu.VMEM((2, 2, blocks, members, 128), F32),
            pltpu.VMEM((2, size, 128), F32),
            pltpu.VMEM((4, members, 128), F32),
            pltpu.VMEM((stages + 1, members, 128), F32),
            pltpu.VMEM((stages, members, 128), F32),
        ] + [pltpu.SMEM(v.shape, v.dtype) for v in smalls] + [pltpu.VMEM((8, cols), F32)] * 3 + [
            dma((blocks,)), dma((10,)), dma((8,)), dma((8,)), dma((10,)), dma((10,)), dma((stages,)), dma((stages,)),
        ],
        compiler_params=pltpu.CompilerParams(
            collective_id=0, has_side_effects=True, vmem_limit_bytes=VLIMIT),
        name="front",
    )(*smalls, state, cr, cc, kk)


def split(x):
    hi = x.astype(BF16)
    return hi, (x - hi.astype(F32)).astype(BF16)


def apply_kernel(adv, anomalies, means, params, final, out, coupling, weights, tapers, lhs1, lhs2, in_sem, out_sem):
    members, lanes = anomalies.shape
    blocks = adv.shape[0]
    cols = blocks * 128
    count = lanes // 2
    width = CHUNK // 128
    fetch = [pltpu.make_async_copy(adv.at[j], out.at[j], in_sem.at[j]) for j in range(blocks)]
    store = [
        pltpu.make_async_copy(out.at[j], final.at[:, pl.ds(j * 128, 128)], out_sem.at[j]) for j in range(blocks)
    ]
    for copy in fetch:
        copy.start()
    row_base = lax.axis_index("gx") * 8
    col_base = lax.axis_index("gy") * cols
    a = anomalies[...]
    mean = means[0:1, :]
    col, rad = params[1:2, :], params[2:3, :]
    obs, err = params[3:4, :], params[4:5, :]
    s2 = jnp.sum(a * a, axis=0, keepdims=True) * (1.0 / (members - 1)) + 1e-05
    inv = 1.0 / (s2 + err)
    shift = s2 * (obs - mean) * inv
    beta = jnp.sqrt(err * inv) - 1.0
    delta = beta * a
    pad = jnp.zeros((lanes - members, lanes), F32)
    at = jnp.concatenate([a, pad], axis=0).T
    g = jnp.dot(at, jnp.concatenate([delta, pad], axis=0), precision=lax.Precision.HIGHEST,
                preferred_element_type=F32)
    ahi, alo = split(a)
    ahi, alo = ahi.astype(F32), alo.astype(F32)
    stacked = jnp.concatenate([ahi, ahi, alo, jnp.zeros_like(alo)], axis=0)
    lhs1[...] = stacked.T.astype(BF16)
    dd = delta + shift
    dhi, dlo = split(dd)
    dhi, dlo = dhi.astype(F32), dlo.astype(F32)
    for b in range(2):
        part = slice(b * count, (b + 1) * count)
        lhs2[b] = jnp.concatenate(
            [dhi[:, part], dhi[:, part], dlo[:, part], jnp.zeros((members, count), F32)], axis=1).astype(BF16)
    pt = jnp.concatenate(
        [params[0:3, :], 1.0 / (s2 * (members - 1)), jnp.zeros((lanes - 4, lanes), F32)], axis=0).T
    lane = lax.broadcasted_iota(jnp.int32, (1, lanes), 1)
    big = 1e9
    low, high = [], []
    for b in range(2):
        inside = (lane >= b * count) & (lane < (b + 1) * count)
        low.append(jnp.min(jnp.where(inside, col - rad, big)))
        high.append(jnp.max(jnp.where(inside, col + rad, -big)))
    for b in range(2):
        @pl.when(((col_base + cols - 1).astype(F32) > low[b]) & (col_base.astype(F32) < high[b]))
        def _(b=b):
            for s in range(b * count, (b + 1) * count):
                first = (s - b * count) // 8 * 8
                coupling[s, first:] = jnp.broadcast_to(
                    g[b * count + first:(b + 1) * count, s:s + 1], (count - first, lanes))
    cells = lax.broadcasted_iota(jnp.int32, (count, CHUNK), 1)
    chunks = cols // CHUNK

    def step(r, chunk):
        start = chunk * CHUNK
        places = [(chunk * width + j, pl.ds(r, members, stride=8)) for j in range(width)]
        first = (col_base + start).astype(F32)
        grow = (row_base + r).astype(F32)
        for b in range(2):
            part = slice(b * count, (b + 1) * count)

            @pl.when((first + (CHUNK - 1.0) > low[b]) & (first < high[b]))
            def _(b=b, part=part):
                x = jnp.concatenate([out[place] for place in places], axis=1)
                dr = pt[part, 0:1] - grow
                dc = (cells + (col_base + start)).astype(F32) - pt[part, 1:2]
                inv2 = 1.0 / (pt[part, 2:3] * pt[part, 2:3])
                t = jnp.maximum(1.0 - (dr * dr + dc * dc) * inv2, 0.0)
                tapers[...] = t * t * pt[part, 3:4]
                xhi, xlo = split(x)
                carried = jnp.dot(
                    lhs1[part, :], jnp.concatenate([xhi, xlo, xhi, jnp.zeros_like(xhi)], axis=0),
                    preferred_element_type=F32)
                groups = [carried[i * 8:(i + 1) * 8, :] for i in range(count // 8)]
                for k in range(count):
                    gi, si = k // 8, k % 8
                    w = groups[gi][si:si + 1, :] * tapers[k:k + 1, :]
                    weights[k:k + 1, :] = w
                    first_group = gi if si < 7 else gi + 1
                    for gj in range(first_group, count // 8):
                        c = coupling[b * count + k, gj * 8:(gj + 1) * 8, :]
                        c = jnp.concatenate([c] * (CHUNK // 128), axis=1)
                        groups[gj] = groups[gj] + c * w
                whi, wlo = split(weights[...])
                x = x + jnp.dot(
                    lhs2[b], jnp.concatenate([whi, wlo, whi, jnp.zeros_like(whi)], axis=0),
                    preferred_element_type=F32)
                for j, place in enumerate(places):
                    out[place] = x[:, j * 128:(j + 1) * 128]

    for chunk in range(chunks):
        mine = range(chunk * width, (chunk + 1) * width)
        for j in mine:
            fetch[j].wait()
        pl.loop(0, 8)(functools.partial(step, chunk=chunk))
        for j in mine:
            store[j].start()
    for copy in store:
        copy.wait()


def apply(adv, anomalies, means, params):
    members, lanes = anomalies.shape
    count = lanes // 2
    vmem = pl.BlockSpec(memory_space=pltpu.VMEM)
    return pl.pallas_call(
        apply_kernel,
        out_shape=jax.ShapeDtypeStruct((adv.shape[1], adv.shape[0] * 128), F32),
        in_specs=[pl.BlockSpec(memory_space=pl.ANY)] + [vmem] * 3,
        out_specs=pl.BlockSpec(memory_space=pl.ANY),
        scratch_shapes=[
            pltpu.VMEM(adv.shape, F32),
            pltpu.VMEM((lanes, count, lanes), F32),
            pltpu.VMEM((count, CHUNK), F32),
            pltpu.VMEM((count, CHUNK), F32),
            pltpu.VMEM((lanes, 256), BF16),
            pltpu.VMEM((2, members, 256), BF16),
            pltpu.SemaphoreType.DMA((adv.shape[0],)),
            pltpu.SemaphoreType.DMA((adv.shape[0],)),
        ],
        compiler_params=pltpu.CompilerParams(vmem_limit_bytes=VLIMIT),
        name="apply",
    )(adv, anomalies, means, params)


def solution(mesh):
    nx, ny = mesh.shape["gx"], mesh.shape["gy"]

    def local(state, cr, cc, kk, owner, trow, tcol, order, radius, obs, err):
        members, rows, cols = state.shape
        smalls = (owner, trow, tcol, order, radius, obs, err)
        adv, anomalies, means, params = front(nx, ny, smalls, state.reshape(members * rows, cols), cr, cc, kk)
        out = apply(adv, anomalies, means, params)
        return out.reshape(members, rows, cols)

    split_spec = P(None, "gx", "gy")
    cell = P("gx", "gy")
    return jax.shard_map(
        local, mesh=mesh, in_specs=(split_spec,) + (cell,) * 3 + (P(),) * 7, out_specs=split_spec, check_vma=False)
```
